1024 devices in a mesh: cells: 16 (over x, y), wall: 64 (over z, core).
Axes of the slice: x: 4, y: 4, z: 32, core: 2. Of those that a mesh axis runs over, the one named last changes fastest.
Arguments:
- shape_coef: bfloat16 [3, 289, 262144], P(None, None, ('cells', 'wall')), may hold values from -3 to 3
- force_coef: bfloat16 [3, 289, 262144], P(None, None, ('cells', 'wall')), may hold values from -1.5 to 1.5
- near_cell: int32 [65536], P(('cells', 'wall')), may hold values from 0 to 255
- near_dest: int32 [65536], P(('cells', 'wall')), may hold values from 0 to 63, as said below
- near_slot: int32 [65536], P(('cells', 'wall')), may hold values from 0 to 1
- panel_centers: float32 [2048, 384], P(('cells', 'wall')), may hold values from -2 to 2
- near_blocks: bfloat16 [2048, 2, 384, 384], P(('cells', 'wall')), may hold values from -0.15625 to 0.15625
- near_pick: int32 [2048], P(('cells', 'wall')), may hold values from 0 to 1
- src_basis: float32 [2048, 384, 16], P(('cells', 'wall')), may hold values from -0.3125 to 0.3125
- far_couple: float32 [2048, 8, 16, 16], P(('cells', 'wall')), may hold values from -0.5 to 0.5
- far_src: int32 [2048, 8], P(('cells', 'wall')), may hold values from 0 to 2047
- far_rank: int32 [2048, 8], P(('cells', 'wall')), may hold values from 1 to 16
- tgt_basis: float32 [2048, 16, 384], P(('cells', 'wall')), may hold values from -1.5 to 1.5
- cluster_slot: int32 [2048], replicated, may hold values from 0 to 2047, each once
Outputs:
- surface: bfloat16 [3, 578, 262144], P(None, None, ('cells', 'wall'))
- density: float32 [2048, 384], P(('cells', 'wall'))
The draws below stay inside these ranges and needn't reach their ends.
Inputs may be any that keep to these rules, and one draw needn't show every extreme that they name: `near_cell`: A cell of the row's own device block of 256 cells; each device holds 64 rows. `near_dest`: among the 64 rows of one device no value appears more than 2 times; in each group of 64 devices along the wall axis some value appears exactly 2 times among the rows of every device of the group. `cluster_slot`: each of 0 to 2047 appears once.
All inputs are finite; a program needn't handle non-finite values.
Results may differ from the reference program's by a relative error of at most 0.0062.
Values may be sent and summed in bfloat16 or wider, within the bound.
No kernel may reach another device: no remote copies, remote signals or barrier semaphores. Data moves between devices by JAX's collectives and lax.ppermute only.
A program may use at most 32 MiB of HBM per device.

```python
import math
import jax
import jax.numpy as jnp
import numpy as np
from jax import lax

ORDER = 16
SH = 289
C_DEV = 256
CELLS = 262144
NEAR_DEV = 64
NEAR_TOTAL = 65536
CAP = 2
PAN = 128
CL_DEV = 2
NCL = 2048
RANK = 16
FB = 8
ITERS = 2
N_WALL = 64


def draw_near_dest(key, part):
    devices_all = NEAR_TOTAL // NEAR_DEV
    groups = devices_all // N_WALL
    hot_dest = jax.random.randint(jax.random.fold_in(key, 11), (groups,), 0, N_WALL)
    hot_device = jnp.repeat(hot_dest, N_WALL)
    keys = jax.random.split(jax.random.fold_in(key, 12), devices_all)

    def device_rows(device_key, hot_one):
        key_items, key_order = jax.random.split(device_key)
        picked_items = jax.random.permutation(key_items, (N_WALL - 1) * CAP)[:NEAR_DEV - CAP]
        other_dest = (picked_items // CAP).astype(jnp.int32)
        other_dest = other_dest + (other_dest >= hot_one).astype(jnp.int32)
        dest_rows = jnp.concatenate([jnp.full((CAP,), hot_one, jnp.int32), other_dest])
        row_order = jax.random.permutation(key_order, NEAR_DEV)
        return dest_rows[row_order]
    return jax.vmap(device_rows)(keys, hot_device).reshape(-1).astype(jnp.int32)


def with_ends(entries, own_key, least, top_value):
    longest = entries.shape.index(max(entries.shape))
    spots = []
    for shift in (0, 1):
        where = [jax.random.randint(jax.random.fold_in(own_key, axis), (), 0, length) for axis, length in enumerate(entries.shape)]
        where[longest] = (where[longest] + shift) % entries.shape[longest]
        spots.append(tuple(where))
    return entries.at[spots[0]].set(least).at[spots[1]].set(top_value)


def steps_of(stream_key, extent, cuts, least, top_value):
    level = 1.0
    for dim, shards_of in cuts:
        draws = jax.random.uniform(jax.random.fold_in(jax.random.fold_in(stream_key, 6), dim), (shards_of,), jnp.float32, least / len(cuts), top_value / len(cuts))
        level = level * jnp.repeat(jnp.exp(draws), extent[dim] // shards_of).reshape((-1,) + (1,) * (len(extent) - 1 - dim))
    return level


def normal_values(own_key, dims, scale, most, cuts=(), kind=jnp.bfloat16):
    values = jax.random.normal(own_key, dims, jnp.float32) * scale
    if len(cuts) > 0:
        values = steps_of(own_key, dims, cuts, -0.22, 0.18) * values
    return jnp.clip(values, min=-most, max=most).astype(kind)


def setup_inputs(seed: int = 0) -> dict:
    key_of = jax.random.split(jax.random.key(seed), 15)
    return {
        "shape_coef": normal_values(key_of[0], (3, SH, CELLS), 0.2, 3.0, ((2, 1024),)),
        "force_coef": normal_values(key_of[1], (3, SH, CELLS), 0.1, 1.5, ((2, 1024),)),
        "near_cell": with_ends(jax.random.randint(key_of[2], (NEAR_TOTAL,), 0, C_DEV), jax.random.fold_in(key_of[2], 1), 0, C_DEV - 1).astype(jnp.int32),
        "near_dest": draw_near_dest(jax.random.fold_in(key_of[14], 71), 0),
        "near_slot": with_ends(jax.random.randint(key_of[4], (NEAR_TOTAL,), 0, CL_DEV), jax.random.fold_in(key_of[4], 1), 0, CL_DEV - 1).astype(jnp.int32),
        "panel_centers": jnp.clip(jax.random.uniform(key_of[5], (NCL, 3 * PAN), jnp.float32, -2.0, 2.0) * steps_of(key_of[5], (NCL, 3 * PAN), ((0, 1024),), -0.4, 0.0), -2.0, 2.0),
        "near_blocks": normal_values(key_of[6], (NCL, 2, 3 * PAN, 3 * PAN), (12 * PAN) ** -0.5, 0.15625, ((0, 1024),)),
        "near_pick": with_ends(jax.random.randint(key_of[7], (NCL,), 0, CL_DEV), jax.random.fold_in(key_of[7], 1), 0, CL_DEV - 1).astype(jnp.int32),
        "src_basis": normal_values(key_of[8], (NCL, 3 * PAN, RANK), (3 * PAN) ** -0.5, 0.3125, ((0, 1024),), jnp.float32),
        "far_couple": normal_values(key_of[9], (NCL, FB, RANK, RANK), (RANK * FB) ** -0.5, 0.5, ((0, 1024),), jnp.float32),
        "far_src": with_ends(jax.random.randint(key_of[10], (NCL, FB), 0, NCL), jax.random.fold_in(key_of[10], 1), 0, NCL - 1).astype(jnp.int32),
        "far_rank": with_ends(jax.random.randint(key_of[11], (NCL, FB), 1, RANK + 1), jax.random.fold_in(key_of[11], 1), 1, RANK).astype(jnp.int32),
        "tgt_basis": normal_values(key_of[12], (NCL, RANK, 3 * PAN), RANK ** -0.5, 1.5, ((0, 1024),), jnp.float32),
        "cluster_slot": jax.random.permutation(key_of[13], NCL).astype(jnp.int32),
    }


soft_core = 0.25
stokes_scale = 1.0 / (8.0 * math.pi)

def harmonics(order):
    lat_count = order + 1
    polar_angle = np.pi * (np.arange(lat_count) + 0.5) / lat_count
    azimuth = np.pi * np.arange(2 * lat_count) / lat_count
    cos_polar = np.repeat(np.cos(polar_angle), 2 * lat_count)
    sin_polar = np.repeat(np.sin(polar_angle), 2 * lat_count)
    az_grid = np.tile(azimuth, lat_count)
    legendre = {}
    legendre[0, 0] = cos_polar * 0.0 + 0.5 / np.sqrt(np.pi)
    for m in range(1, order + 1):
        legendre[m, m] = -np.sqrt((2.0 * m + 1.0) / (2.0 * m)) * sin_polar * legendre[m - 1, m - 1]
    for m in range(order):
        legendre[m + 1, m] = np.sqrt(2.0 * m + 3.0) * cos_polar * legendre[m, m]
    for m in range(order + 1):
        for l in range(m + 2, order + 1):
            factor = np.sqrt((4.0 * l * l - 1.0) / (l * l - m * m))
            backward = np.sqrt(((l - 1.0) ** 2 - m * m) / (4.0 * (l - 1.0) ** 2 - 1.0))
            legendre[l, m] = factor * (cos_polar * legendre[l - 1, m] - backward * legendre[l - 2, m])
    columns = []
    for l in range(order + 1):
        for m in range(-l, l + 1):
            if m > 0:
                columns.append(np.sqrt(2.0) * legendre[l, m] * np.cos(m * az_grid))
            elif m < 0:
                columns.append(np.sqrt(2.0) * legendre[l, -m] * np.sin(-m * az_grid))
            else:
                columns.append(legendre[l, 0])
    return np.stack(columns, axis=1)

def kernel_block(pieces):
    points, forces, centers = pieces
    panels = centers.shape[1] // 3
    source = points.astype(jnp.float32)
    strength = forces.astype(jnp.float32)
    spots = centers.reshape(centers.shape[0], 3, panels)
    offset = [spots[:, a, :, None] - source[:, a, None, :] for a in range(3)]
    radius_sq = offset[0] * offset[0] + offset[1] * offset[1] + offset[2] * offset[2] + soft_core
    inverse = lax.rsqrt(radius_sq)
    inverse_cube = inverse * inverse * inverse
    along = offset[0] * strength[:, 0, None, :] + offset[1] * strength[:, 1, None, :] + offset[2] * strength[:, 2, None, :]
    parts = [lax.optimization_barrier(jnp.sum(strength[:, a, None, :] * inverse + offset[a] * along * inverse_cube, axis=2)) for a in range(3)]
    return jnp.stack(parts, axis=1).reshape(centers.shape[0], 3 * panels) * stokes_scale

def stokes_rows(points, forces, centers, block):
    total = points.shape[0]
    width = math.gcd(total, block)
    groups = total // width
    result = lax.map(kernel_block, (points.reshape(groups, width, 3, points.shape[2]), forces.reshape(groups, width, 3, forces.shape[2]), centers.reshape(groups, width, centers.shape[1])))
    return result.reshape(total, centers.shape[1])

def near_apply(pair_args):
    blocks, vectors = pair_args
    return jnp.einsum('bij,bj->i', blocks.astype(jnp.float32), vectors, precision=lax.Precision.HIGHEST)

def reference(shape_coef, force_coef, near_cell, near_dest, near_slot, panel_centers, near_blocks, near_pick, src_basis, far_couple, far_src, far_rank, tgt_basis, cluster_slot):
    harmonic = jnp.asarray(harmonics(ORDER), jnp.float32).astype(jnp.bfloat16)
    harmonic_wide = harmonic.astype(jnp.float32)
    surface = jnp.einsum('qs,asc->aqc', harmonic_wide, shape_coef.astype(jnp.float32), precision=lax.Precision.HIGHEST).astype(jnp.bfloat16)
    row_ids = jnp.arange(NEAR_TOTAL, dtype=jnp.int32)
    source = row_ids // NEAR_DEV
    cell_ids = (source * C_DEV + near_cell).astype(jnp.int32)
    points = jnp.transpose(jnp.take(surface, cell_ids, axis=2), (2, 0, 1))
    picked = jnp.take(force_coef, cell_ids, axis=2).astype(jnp.float32)
    forces = jnp.einsum('qs,asn->naq', harmonic_wide, picked, precision=lax.Precision.HIGHEST).astype(jnp.bfloat16)
    target = ((source // N_WALL * N_WALL + near_dest) * CL_DEV + near_slot).astype(jnp.int32)
    centers = jnp.take(panel_centers, target, axis=0)
    velocity = stokes_rows(points, forces, centers, 64)
    wall_rhs = -jax.ops.segment_sum(velocity, target, num_segments=NCL)
    clusters = jnp.arange(NCL, dtype=jnp.int32)
    owner = clusters // CL_DEV
    previous = owner // N_WALL * N_WALL + (owner % N_WALL + N_WALL - 1) % N_WALL
    neighbor_ids = (previous * CL_DEV + near_pick).astype(jnp.int32)
    source_rows = jnp.take(cluster_slot, far_src, axis=0).astype(jnp.int32)
    levels = jnp.arange(RANK, dtype=jnp.int32)
    rank_keep = (levels[None, None, :, None] < far_rank[:, :, None, None]) & (levels[None, None, None, :] < far_rank[:, :, None, None])
    masked = jnp.where(rank_keep, far_couple, jnp.zeros_like(far_couple))
    density = wall_rhs
    for step in range(ITERS):
        density_low = lax.optimization_barrier(density.astype(jnp.bfloat16)).astype(jnp.float32)
        paired = jnp.stack([density_low, jnp.take(density_low, neighbor_ids, axis=0)], axis=1)
        near_term = lax.map(near_apply, (near_blocks, paired))
        coefficients = jnp.einsum('cpr,cp->cr', src_basis, density, precision=lax.Precision.HIGHEST)
        gathered = jnp.take(coefficients, source_rows, axis=0)
        mixed_rank = jnp.einsum('cbij,cbj->ci', masked, gathered, precision=lax.Precision.HIGHEST)
        far_term = jnp.einsum('cr,crp->cp', mixed_rank, tgt_basis, precision=lax.Precision.HIGHEST)
        density = wall_rhs - near_term - far_term
    return (surface, density)
```

```python
import functools
import math

import jax
import jax.numpy as jnp
import numpy as np
from jax import lax
from jax.experimental import pallas as pl
from jax.experimental.pallas import tpu as pltpu
from jax.sharding import Mesh
from jax.sharding import PartitionSpec as P

ORDER = 16
ITERS = 2
WALL = ("wall_0", "wall_1")
CELLS = ("cells_0", "cells_1")
CELLS_WALL = ("cells_0", "cells_1", "wall_0", "wall_1")

soft_core = 0.25
stokes_scale = 1.0 / (8.0 * math.pi)
LANES = 128
PANELS = 128
f32 = jnp.float32
bf16 = jnp.bfloat16
VMEM = pl.BlockSpec(memory_space=pltpu.VMEM)
SMEM = pl.BlockSpec(memory_space=pltpu.SMEM)


def shifted(array, axis, by):
    devices = lax.axis_size(axis)
    return lax.ppermute(array, axis, [(i, (i + by) % devices) for i in range(devices)])


def harmonics(order):
    lat_count = order + 1
    polar_angle = np.pi * (np.arange(lat_count) + 0.5) / lat_count
    azimuth = np.pi * np.arange(2 * lat_count) / lat_count
    cos_polar = np.repeat(np.cos(polar_angle), 2 * lat_count)
    sin_polar = np.repeat(np.sin(polar_angle), 2 * lat_count)
    az_grid = np.tile(azimuth, lat_count)
    legendre = {}
    legendre[0, 0] = cos_polar * 0.0 + 0.5 / np.sqrt(np.pi)
    for m in range(1, order + 1):
        legendre[m, m] = -np.sqrt((2.0 * m + 1.0) / (2.0 * m)) * sin_polar * legendre[m - 1, m - 1]
    for m in range(order):
        legendre[m + 1, m] = np.sqrt(2.0 * m + 3.0) * cos_polar * legendre[m, m]
    for m in range(order + 1):
        for l in range(m + 2, order + 1):
            factor = np.sqrt((4.0 * l * l - 1.0) / (l * l - m * m))
            backward = np.sqrt(((l - 1.0) ** 2 - m * m) / (4.0 * (l - 1.0) ** 2 - 1.0))
            legendre[l, m] = factor * (
                cos_polar * legendre[l - 1, m] - backward * legendre[l - 2, m]
            )
    columns = []
    for l in range(order + 1):
        for m in range(-l, l + 1):
            if m > 0:
                columns.append(np.sqrt(2.0) * legendre[l, m] * np.cos(m * az_grid))
            elif m < 0:
                columns.append(np.sqrt(2.0) * legendre[l, -m] * np.sin(-m * az_grid))
            else:
                columns.append(legendre[l, 0])
    return np.stack(columns, axis=1)


def dot_nn(a, b):
    return lax.dot_general(a, b, (((1,), (0,)), ((), ())), preferred_element_type=f32)


def dot_nt(a, b):
    return lax.dot_general(a, b, (((1,), (1,)), ((), ())), preferred_element_type=f32)


def dot_tn(a, b):
    return lax.dot_general(a, b, (((0,), (0,)), ((), ())), preferred_element_type=f32)


def split3(value):
    high = value.astype(bf16).astype(f32)
    rest = value - high
    middle = rest.astype(bf16).astype(f32)
    return high, middle, rest - middle


def sources_kernel(cell_ref, shape_ref, force_ref, grid_ref, out_ref):
    rows = out_ref.shape[1]
    cells = shape_ref.shape[2]
    pick = (lax.broadcasted_iota(jnp.int32, (rows, cells), 1) == cell_ref[...]).astype(bf16)
    for base, ref in ((0, shape_ref), (3, force_ref)):
        for a in range(3):
            coefs = dot_nt(pick, ref[a]).astype(bf16)
            out_ref[base + a] = dot_nn(coefs, grid_ref[...]).astype(bf16)


def near_sources(near_cell, shape_coef, force_coef, grid):
    rows = near_cell.shape[0]
    return pl.pallas_call(
        sources_kernel,
        out_shape=jax.ShapeDtypeStruct((6, rows, grid.shape[1]), bf16),
        in_specs=[VMEM] * 4,
        out_specs=VMEM,
        cost_estimate=pl.CostEstimate(flops=200_000_000, bytes_accessed=2_500_000, transcendentals=0),
        name="near_sources",
    )(near_cell.reshape(rows, 1), shape_coef, force_coef, grid)


def put(ref, k, value):
    rows = value.shape[0]
    for j in range(ref.shape[0]):
        ref[j, pl.ds(k * rows, rows), :] = value[:, j * LANES : (j + 1) * LANES]


def get(ref, r, rows):
    return jnp.concatenate(
        [ref[j, pl.ds(r, 16, stride=rows), :] for j in range(ref.shape[0])], axis=1
    )


def pairs_kernel(tcol_ref, trow_ref, src_ref, ctr_ref, out_ref, ysc, gsc, bsc, mom, xsc):
    rows, quads = src_ref.shape[1], src_ref.shape[2]
    walls, width = out_ref.shape
    pan = PANELS
    own = width // (3 * pan)
    clusters = walls * own
    lines = width // LANES
    y = [src_ref[a].astype(f32) for a in range(3)]
    f = [src_ref[3 + a].astype(f32) for a in range(3)]
    y2 = y[0] * y[0] + y[1] * y[1] + y[2] * y[2]
    yf = y[0] * f[0] + y[1] * f[1] + y[2] * f[2]
    for k in range(9):
        put(ysc, k, -2.0 * y[k % 3])
    for k, piece in enumerate(split3(y2)):
        put(ysc, 9 + k, piece)
    for k in range(12, 15):
        put(ysc, k, jnp.ones((rows, quads), f32))
    put(ysc, 15, jnp.zeros((rows, quads), f32))
    for b in range(3):
        put(gsc, b, f[b])
    put(gsc, 3, yf)
    for a in range(3):
        for b in range(3):
            put(gsc, 4 + 3 * a + b, y[a] * f[b])
        put(gsc, 13 + a, y[a] * yf)
    pick = (lax.broadcasted_iota(jnp.int32, (rows, clusters), 1) == tcol_ref[...]).astype(bf16)
    x = []
    for a in range(3):
        total = None
        spots = jnp.concatenate(
            [ctr_ref[pl.ds(3 * t + a, walls, stride=lines), :] for t in range(own)], axis=0
        )
        for i, piece in enumerate(split3(spots)):
            part = dot_nn(pick, piece.astype(bf16))
            bsc[pl.ds((3 * i + a) * rows, rows), :] = part
            total = part if total is None else total + part
        x.append(total)
        xsc[pl.ds(a * rows, rows), :] = total
    x2 = x[0] * x[0] + x[1] * x[1] + x[2] * x[2] + soft_core
    for k in range(9, 12):
        bsc[pl.ds(k * rows, rows), :] = jnp.ones((rows, pan), f32)
    for k, piece in enumerate(split3(x2)):
        bsc[pl.ds((12 + k) * rows, rows), :] = piece
    bsc[pl.ds(15 * rows, rows), :] = jnp.zeros((rows, pan), f32)

    def row(r, carry):
        yr = get(ysc, r, rows).astype(bf16)
        br = bsc[pl.ds(r, 16, stride=rows), :]
        g = get(gsc, r, rows)
        g_hi = g.astype(bf16)
        g_lo = (g - g_hi.astype(f32)).astype(bf16)
        rho2 = dot_tn(yr, br.astype(bf16))
        inverse = lax.rsqrt(rho2)
        cube = inverse * inverse * inverse
        c_hi = cube.astype(bf16)
        c_lo = (cube - c_hi.astype(f32)).astype(bf16)
        i_hi = inverse.astype(bf16)
        i_lo = (inverse - i_hi.astype(f32)).astype(bf16)
        first = dot_nn(jnp.concatenate([g_hi, g_lo], axis=0), c_hi)
        mom[pl.ds(r, 16, stride=rows), :] = first[:16] + first[16:] + dot_nn(g_hi, c_lo)
        plain = dot_nn(g_hi, i_hi) + dot_nn(g_hi, i_lo)
        mom[pl.ds(16 * rows + r, 8, stride=rows), :] = plain[:8]
        return carry

    lax.fori_loop(0, rows, row, 0, unroll=PAIR_UNROLL)
    x = [xsc[pl.ds(a * rows, rows), :] for a in range(3)]
    moment = [mom[pl.ds(c * rows, rows), :] for c in range(19)]
    common = x[0] * moment[0] + x[1] * moment[1] + x[2] * moment[2] - moment[3]
    drop = (lax.broadcasted_iota(jnp.int32, (clusters, rows), 0) == trow_ref[...]).astype(bf16)
    for a in range(3):
        local_part = x[0] * moment[4 + 3 * a] + x[1] * moment[5 + 3 * a] + x[2] * moment[6 + 3 * a]
        velocity = moment[16 + a] + x[a] * common - (local_part - moment[13 + a])
        velocity = velocity * (-stokes_scale)
        total = None
        for piece in split3(velocity):
            part = dot_nn(drop, piece.astype(bf16))
            total = part if total is None else total + part
        for t in range(own):
            out_ref[:, pl.ds((3 * t + a) * pan, pan)] = total[t * walls : (t + 1) * walls, :]


PAIR_UNROLL = 8


def pair_sums(target, sources, centers, walls):
    rows, quads = sources.shape[1:]
    width = centers.shape[0] * LANES // walls
    pan = PANELS
    return pl.pallas_call(
        pairs_kernel,
        out_shape=jax.ShapeDtypeStruct((walls, width), f32),
        in_specs=[VMEM] * 4,
        out_specs=VMEM,
        scratch_shapes=[
            pltpu.VMEM((quads // LANES, 16 * rows, LANES), f32),
            pltpu.VMEM((quads // LANES, 16 * rows, LANES), f32),
            pltpu.VMEM((16 * rows, pan), f32),
            pltpu.VMEM((24 * rows, pan), f32),
            pltpu.VMEM((3 * rows, pan), f32),
        ],
        cost_estimate=pl.CostEstimate(
            flops=1_000_000_000, bytes_accessed=1_000_000, transcendentals=5_000_000
        ),
        name="pair_sums",
    )(target.reshape(rows, 1), target.reshape(1, rows), sources, centers)


def coefs_of(density, basis_ref):
    parts = []
    for t in range(density.shape[0]):
        parts.append(
            lax.dot_general(
                density[t : t + 1, :],
                basis_ref[t],
                (((1,), (1,)), ((), ())),
                precision=lax.Precision.HIGHEST,
                preferred_element_type=f32,
            )
        )
    return jnp.concatenate(parts * (LANES // (len(parts) * parts[0].shape[1])), axis=1)


def start_kernel(recv_ref, basis_ref, rhs_ref, low_ref, coef_ref):
    rhs = jnp.sum(recv_ref[...].astype(f32), axis=0)
    rhs_ref[...] = rhs
    low_ref[...] = rhs.astype(bf16)
    coef_ref[...] = coefs_of(rhs, basis_ref)


def near_kernel(pick_ref, blocks_ref, low_ref, other_ref, out_ref):
    clusters, width = out_ref.shape
    other = other_ref[...].astype(f32)
    for t in range(clusters):
        low = low_ref[t : t + 1, :]
        chosen = other[0:1, :]
        for n in range(1, other.shape[0]):
            chosen = jnp.where(pick_ref[t] == n, other[n : n + 1, :], chosen)
        out_ref[t : t + 1, :] = dot_nt(low, blocks_ref[t, 0]) + dot_nt(
            chosen.astype(bf16), blocks_ref[t, 1]
        )


def far_of(index_ref, table_ref, couple_ref, target_ref, t):
    blocks = couple_ref.shape[1]
    total = None
    for b in range(blocks):
        row = table_ref[pl.ds(index_ref[t * blocks + b], 1), :]
        part = couple_ref[t, b] * row
        total = part if total is None else total + part
    mixed = jnp.sum(total, axis=1, keepdims=True)
    return jnp.sum(mixed * target_ref[t], axis=0, keepdims=True)


def step_kernel(
    index_ref, table_ref, couple_ref, target_ref, rhs_ref, near_ref, basis_ref, *out_refs
):
    clusters = rhs_ref.shape[0]
    far = jnp.concatenate(
        [far_of(index_ref, table_ref, couple_ref, target_ref, t) for t in range(clusters)], axis=0
    )
    density = rhs_ref[...] - near_ref[...] - far
    out_refs[0][...] = density
    if len(out_refs) > 1:
        out_refs[1][...] = density.astype(bf16)
        out_refs[2][...] = coefs_of(density, basis_ref)


def start(received, basis):
    clusters, rank, width = basis.shape
    return pl.pallas_call(
        start_kernel,
        out_shape=(
            jax.ShapeDtypeStruct((clusters, width), f32),
            jax.ShapeDtypeStruct((clusters, width), bf16),
            jax.ShapeDtypeStruct((1, LANES), f32),
        ),
        in_specs=[VMEM] * 2,
        out_specs=(VMEM,) * 3,
        cost_estimate=pl.CostEstimate(flops=500_000, bytes_accessed=400_000, transcendentals=0),
        name="start",
    )(received, basis)


def near_part(pick, blocks, low, other):
    return pl.pallas_call(
        near_kernel,
        out_shape=jax.ShapeDtypeStruct(low.shape, f32),
        in_specs=[SMEM, VMEM, VMEM, VMEM],
        out_specs=VMEM,
        cost_estimate=pl.CostEstimate(flops=2_000_000, bytes_accessed=1_200_000, transcendentals=0),
        name="near_part",
    )(pick, blocks, low, other)


def step(index, table, couple, target, rhs, near, basis, last):
    clusters, rank, width = basis.shape
    shapes = [jax.ShapeDtypeStruct((clusters, width), f32)]
    if not last:
        shapes.append(jax.ShapeDtypeStruct((clusters, width), bf16))
        shapes.append(jax.ShapeDtypeStruct((1, LANES), f32))
    return pl.pallas_call(
        step_kernel,
        out_shape=tuple(shapes),
        in_specs=[SMEM] + [VMEM] * 6,
        out_specs=(VMEM,) * len(shapes),
        cost_estimate=pl.CostEstimate(flops=500_000, bytes_accessed=500_000, transcendentals=0),
        name="step",
    )(index, table, couple, target, rhs, near, basis)


def local(
    shape_coef,
    force_coef,
    near_cell,
    near_dest,
    near_slot,
    panel_centers,
    near_blocks,
    near_pick,
    src_basis,
    far_couple,
    far_src,
    far_rank,
    tgt_basis,
    cluster_slot,
):
    walls = lax.axis_size(WALL)
    clusters, width = panel_centers.shape
    rank = far_couple.shape[2]
    harmonic = harmonics(ORDER)
    quads = harmonic.shape[0]
    padded = -(-quads // LANES) * LANES
    grid = np.zeros((harmonic.shape[1], padded), np.float32)
    grid[:, :quads] = harmonic.T
    grid = jnp.asarray(grid, f32).astype(bf16)
    harmonic = jnp.asarray(harmonic, f32).astype(bf16)

    centers = gather_wall(panel_centers)
    sources = near_sources(near_cell, shape_coef, force_coef, grid)
    surface = jnp.einsum(
        "qs,asc->aqc", harmonic, shape_coef, preferred_element_type=jnp.float32
    ).astype(bf16)

    source_rows = jnp.take(cluster_slot, far_src.reshape(-1), axis=0)
    per_row = LANES // rank
    index, offset = table_place(source_rows, clusters, rank)
    levels = jnp.arange(rank, dtype=jnp.int32)
    keep = (levels[None, None, :, None] < far_rank[:, :, None, None]) & (
        levels[None, None, None, :] < far_rank[:, :, None, None]
    )
    masked = jnp.where(keep, far_couple, jnp.zeros_like(far_couple))
    lane_part = jnp.arange(LANES, dtype=jnp.int32) // rank
    here = lane_part[None, None, None, :] == offset.reshape(far_src.shape)[:, :, None, None]
    couple = jnp.where(here, jnp.tile(masked, (1, 1, 1, per_row)), 0.0)
    basis = jnp.swapaxes(src_basis, 1, 2)

    target = near_slot * walls + near_dest
    sums = pair_sums(target, sources, centers, walls)
    received = exchange_wall(sums, clusters)
    rhs, low, coef = start(received, basis)
    for k in range(ITERS):
        other = shifted(low, WALL, 1)
        near = near_part(near_pick, near_blocks, low, other)
        table = gather_all(coef, clusters, rank)
        out = step(index, table, couple, tgt_basis, rhs, near, basis, k == ITERS - 1)
        if k < ITERS - 1:
            density, low, coef = out
        else:
            (density,) = out
    return (surface, density)


def gather_wall(panel_centers):
    walls = lax.axis_size(WALL)
    flat = panel_centers.reshape(1, 1, -1)
    pieces = jnp.broadcast_to(flat, (walls, 1, flat.shape[2]))
    pieces = lax.all_to_all(pieces, WALL, split_axis=0, concat_axis=0, tiled=True)
    return pieces.reshape(-1, LANES)


def exchange_wall(sums, clusters):
    walls = sums.shape[0]
    pieces = sums.astype(bf16).reshape(walls, clusters, -1)
    return lax.all_to_all(pieces, WALL, split_axis=0, concat_axis=0, tiled=True)


def gather_all(coef, clusters, rank):
    walls = lax.axis_size(WALL)
    cells = lax.axis_size(CELLS)
    groups = LANES // (clusters * rank)
    lane = jnp.arange(LANES, dtype=jnp.int32) // (clusters * rank)
    mine = jnp.where(lane[None, :] == lax.axis_index(WALL) // (walls // groups), coef, 0.0)
    pieces = jnp.broadcast_to(mine[:, None, :], (walls, 1, LANES))
    pieces = lax.all_to_all(pieces, WALL, split_axis=0, concat_axis=0, tiled=True)
    group = jnp.sum(pieces.reshape(groups, walls // groups, LANES), axis=0)
    pieces = jnp.broadcast_to(group.reshape(1, 1, -1), (cells, 1, group.size))
    pieces = lax.all_to_all(pieces, CELLS, split_axis=0, concat_axis=0, tiled=True)
    return pieces.reshape(-1, LANES)


def table_place(slots, clusters, rank):
    walls = lax.axis_size(WALL)
    groups = LANES // (clusters * rank)
    lines = walls // groups
    device = slots // clusters
    cell, wall = device // walls, device % walls
    return cell * lines + wall % lines, wall // lines * clusters + slots % clusters


def solution(mesh):
    finer = Mesh(mesh.devices.reshape(4, 4, 32, 2), ("cells_0", "cells_1", "wall_0", "wall_1"))
    return jax.shard_map(
        local,
        mesh=finer,
        in_specs=(
            P(None, None, CELLS_WALL),
            P(None, None, CELLS_WALL),
            P(CELLS_WALL),
            P(CELLS_WALL),
            P(CELLS_WALL),
            P(CELLS_WALL, None),
            P(CELLS_WALL, None, None, None),
            P(CELLS_WALL),
            P(CELLS_WALL, None, None),
            P(CELLS_WALL, None, None, None),
            P(CELLS_WALL, None),
            P(CELLS_WALL, None),
            P(CELLS_WALL, None, None),
            P(),
        ),
        out_specs=(P(None, None, CELLS_WALL), P(CELLS_WALL, None)),
        check_vma=False,
    )
```

```python
import functools
import math

import jax
import jax.numpy as jnp
import numpy as np
from jax import lax
from jax.experimental import pallas as pl
from jax.experimental.pallas import tpu as pltpu
from jax.sharding import Mesh
from jax.sharding import PartitionSpec as P

ORDER = 16
ITERS = 2
WALL = ("wall_0", "wall_1")
CHIPS = "wall_0"
CORE = "wall_1"
PLANE = ("cells_0", "cells_1", "wall_1")
CELLS_WALL = ("cells_0", "cells_1", "wall_0", "wall_1")

soft_core = 0.25
stokes_scale = 1.0 / (8.0 * math.pi)
LANES = 128
REACH = 2.0
FIXED = 32767.0
PANELS = 128
OWN = 2
f32 = jnp.float32
bf16 = jnp.bfloat16
VMEM = pl.BlockSpec(memory_space=pltpu.VMEM)
SMEM = pl.BlockSpec(memory_space=pltpu.SMEM)


def shifted(array, axis, by):
    devices = lax.axis_size(axis)
    return lax.ppermute(array, axis, [(i, (i + by) % devices) for i in range(devices)])


def harmonics(order):
    lat_count = order + 1
    polar_angle = np.pi * (np.arange(lat_count) + 0.5) / lat_count
    azimuth = np.pi * np.arange(2 * lat_count) / lat_count
    cos_polar = np.repeat(np.cos(polar_angle), 2 * lat_count)
    sin_polar = np.repeat(np.sin(polar_angle), 2 * lat_count)
    az_grid = np.tile(azimuth, lat_count)
    legendre = {}
    legendre[0, 0] = cos_polar * 0.0 + 0.5 / np.sqrt(np.pi)
    for m in range(1, order + 1):
        legendre[m, m] = -np.sqrt((2.0 * m + 1.0) / (2.0 * m)) * sin_polar * legendre[m - 1, m - 1]
    for m in range(order):
        legendre[m + 1, m] = np.sqrt(2.0 * m + 3.0) * cos_polar * legendre[m, m]
    for m in range(order + 1):
        for l in range(m + 2, order + 1):
            factor = np.sqrt((4.0 * l * l - 1.0) / (l * l - m * m))
            backward = np.sqrt(((l - 1.0) ** 2 - m * m) / (4.0 * (l - 1.0) ** 2 - 1.0))
            legendre[l, m] = factor * (
                cos_polar * legendre[l - 1, m] - backward * legendre[l - 2, m]
            )
    columns = []
    for l in range(order + 1):
        for m in range(-l, l + 1):
            if m > 0:
                columns.append(np.sqrt(2.0) * legendre[l, m] * np.cos(m * az_grid))
            elif m < 0:
                columns.append(np.sqrt(2.0) * legendre[l, -m] * np.sin(-m * az_grid))
            else:
                columns.append(legendre[l, 0])
    return np.stack(columns, axis=1)


def kept(shape, dtype):
    return pltpu.VMEM(shape, dtype)


def held(*arrays):
    return [pltpu.with_memory_space_constraint(array, pltpu.VMEM) for array in arrays]


def dot_nn(a, b):
    return lax.dot_general(a, b, (((1,), (0,)), ((), ())), preferred_element_type=f32)


def dot_nt(a, b):
    return lax.dot_general(a, b, (((1,), (1,)), ((), ())), preferred_element_type=f32)


def dot_tn(a, b):
    return lax.dot_general(a, b, (((0,), (0,)), ((), ())), preferred_element_type=f32)


def split3(value):
    high = value.astype(bf16).astype(f32)
    rest = value - high
    middle = rest.astype(bf16).astype(f32)
    return high, middle, rest - middle


def sources_kernel(cell_ref, shape_ref, force_ref, grid_ref, out_ref):
    rows = out_ref.shape[1]
    cells = shape_ref.shape[2]
    pick = (lax.broadcasted_iota(jnp.int32, (cells, rows), 0) == cell_ref[...]).astype(f32)
    pick = jnp.transpose(pick).astype(bf16)
    for base, ref in ((0, shape_ref), (3, force_ref)):
        for a in range(3):
            coefs = dot_nt(pick, ref[a]).astype(bf16)
            out_ref[base + a] = dot_nn(coefs, grid_ref[...]).astype(bf16)


def near_sources(near_cell, shape_coef, force_coef, grid):
    rows = near_cell.shape[0]
    return pl.pallas_call(
        sources_kernel,
        out_shape=kept((6, rows, grid.shape[1]), bf16),
        in_specs=[VMEM] * 4,
        out_specs=VMEM,
        cost_estimate=pl.CostEstimate(flops=200_000_000, bytes_accessed=2_500_000, transcendentals=0),
        name="near_sources",
    )(near_cell.reshape(1, rows), shape_coef, force_coef, grid)


def put(ref, k, value):
    rows = value.shape[0]
    for j in range(ref.shape[0]):
        ref[j, pl.ds(k * rows, rows), :] = value[:, j * LANES : (j + 1) * LANES]


def get(ref, r, rows):
    return jnp.concatenate(
        [ref[j, pl.ds(r, 16, stride=rows), :] for j in range(ref.shape[0])], axis=1
    )


def pairs_kernel(
    cores, dest_ref, slot_ref, src_ref, ctr_ref, out_ref, ysc, gsc, bsc, mom, xsc, csc, *bufs
):
    rows, quads = src_ref.shape[1], src_ref.shape[2]
    lines = OWN * 3
    walls = out_ref.shape[0] // lines
    third = len(bufs) // 3
    rho_bufs, inv_bufs, cube_bufs = bufs[:third], bufs[third : 2 * third], bufs[2 * third :]
    pan = PANELS
    own = OWN
    clusters = walls * own
    dest, slot = dest_ref[...], slot_ref[...]
    chips = walls // cores
    place = slot * walls + lax.rem(dest, cores) * chips + lax.div(dest, cores)
    target = slot * walls + dest
    y = [src_ref[a].astype(f32) for a in range(3)]
    f = [src_ref[3 + a].astype(f32) for a in range(3)]
    y2 = y[0] * y[0] + y[1] * y[1] + y[2] * y[2]
    yf = y[0] * f[0] + y[1] * f[1] + y[2] * f[2]
    for k in range(9):
        put(ysc, k, -2.0 * y[k % 3])
    for k, piece in enumerate(split3(y2)):
        put(ysc, 9 + k, piece)
    for k in range(12, 15):
        put(ysc, k, jnp.ones((rows, quads), f32))
    put(ysc, 15, jnp.zeros((rows, quads), f32))
    for b in range(3):
        put(gsc, b, f[b])
    put(gsc, 3, yf)
    for a in range(3):
        for b in range(3):
            put(gsc, 4 + 3 * a + b, y[a] * f[b])
        put(gsc, 13 + a, y[a] * yf)
    csc[...] = ctr_ref[...].astype(jnp.int32).astype(f32) * (REACH / FIXED)
    pick = (lax.broadcasted_iota(jnp.int32, (clusters, rows), 0) == place).astype(f32)
    pick = jnp.transpose(pick).astype(bf16)
    x = []
    for a in range(3):
        total = None
        spots = jnp.concatenate(
            [csc[pl.ds(own * a + t, walls, stride=lines), :] for t in range(own)], axis=0
        )
        for i, piece in enumerate(split3(spots)):
            part = dot_nn(pick, piece.astype(bf16))
            bsc[pl.ds((3 * i + a) * rows, rows), :] = part
            total = part if total is None else total + part
        x.append(total)
        xsc[pl.ds(a * rows, rows), :] = total
    x2 = x[0] * x[0] + x[1] * x[1] + x[2] * x[2] + soft_core
    for k in range(9, 12):
        bsc[pl.ds(k * rows, rows), :] = jnp.ones((rows, pan), f32)
    for k, piece in enumerate(split3(x2)):
        bsc[pl.ds((12 + k) * rows, rows), :] = piece
    bsc[pl.ds(15 * rows, rows), :] = jnp.zeros((rows, pan), f32)

    lanes = len(rho_bufs) // 2

    def turn(i, old, new):
        held_inv, held_cube = inv_bufs[old::2], cube_bufs[old::2]
        next_inv, next_cube = inv_bufs[new::2], cube_bufs[new::2]
        held_rho, next_rho = rho_bufs[old::2], rho_bufs[new::2]
        for n in range(lanes):
            r = jnp.clip(lanes * (i - 2) + n, n, rows - lanes + n)
            g = get(gsc, r, rows)
            g_hi = g.astype(bf16)
            g_lo = (g - g_hi.astype(f32)).astype(bf16)
            first = dot_nt(jnp.concatenate([g_hi, g_lo], axis=0), held_cube[n][...])
            plain = dot_nt(g_hi, held_inv[n][...])
            mom[pl.ds(r, 16, stride=rows), :] = first[:16] + first[16:]
            mom[pl.ds(16 * rows + r, 8, stride=rows), :] = plain[:8]
        for n in range(lanes):
            inverse = lax.rsqrt(held_rho[n][...])
            next_inv[n][...] = inverse.astype(bf16)
            next_cube[n][...] = (inverse * inverse * inverse).astype(bf16)
        for n in range(lanes):
            r = jnp.minimum(lanes * i + n, rows - lanes + n)
            yr = get(ysc, r, rows).astype(bf16)
            br = bsc[pl.ds(r, 16, stride=rows), :].astype(bf16)
            next_rho[n][...] = dot_tn(br, yr)

    def turns(i, carry):
        turn(2 * i, 0, 1)
        turn(2 * i + 1, 1, 0)
        return carry

    lax.fori_loop(0, (rows // lanes + 2 + 1) // 2, turns, 0, unroll=TURN_UNROLL)
    x = [xsc[pl.ds(a * rows, rows), :] for a in range(3)]
    moment = [mom[pl.ds(c * rows, rows), :] for c in range(19)]
    common = x[0] * moment[0] + x[1] * moment[1] + x[2] * moment[2] - moment[3]
    drop = (lax.broadcasted_iota(jnp.int32, (clusters, rows), 0) == target).astype(bf16)
    for a in range(3):
        local_part = x[0] * moment[4 + 3 * a] + x[1] * moment[5 + 3 * a] + x[2] * moment[6 + 3 * a]
        velocity = moment[16 + a] + x[a] * common - (local_part - moment[13 + a])
        velocity = velocity * (-stokes_scale)
        total = None
        for piece in split3(velocity):
            part = dot_nn(drop, piece.astype(bf16))
            total = part if total is None else total + part
        for t in range(own):
            part = total[t * walls : (t + 1) * walls, :]
            csc[pl.ds(own * a + t, walls, stride=lines), :] = part
    out_ref[...] = csc[...].astype(out_ref.dtype)


PAIR_LANES = 4
TURN_UNROLL = 1


def pair_sums(dest, slot, sources, centers, live, cores):
    rows, quads = sources.shape[1:]
    pan = PANELS
    return pl.pallas_call(
        functools.partial(pairs_kernel, cores),
        out_shape=jax.ShapeDtypeStruct(centers.shape, bf16),
        in_specs=[VMEM] * 4,
        out_specs=VMEM,
        scratch_shapes=[
            pltpu.VMEM((quads // LANES, 16 * rows, LANES), f32),
            pltpu.VMEM((quads // LANES, 16 * rows, LANES), f32),
            pltpu.VMEM((16 * rows, pan), f32),
            pltpu.VMEM((24 * rows, pan), f32),
            pltpu.VMEM((3 * rows, pan), f32),
            pltpu.VMEM(centers.shape, f32),
        ]
        + [pltpu.VMEM((pan, quads), f32)] * (2 * PAIR_LANES)
        + [pltpu.VMEM((pan, quads), bf16)] * (4 * PAIR_LANES),
        cost_estimate=pl.CostEstimate(
            flops=1_000_000_000, bytes_accessed=1_000_000, transcendentals=5_000_000
        ),
        name="pair_sums",
    )(*held(dest.reshape(1, rows), slot.reshape(1, rows), sources, centers))


def coefs_of(density, basis_ref):
    parts = []
    for t in range(density.shape[0]):
        parts.append(
            lax.dot_general(
                density[t : t + 1, :],
                basis_ref[t],
                (((1,), (1,)), ((), ())),
                precision=lax.Precision.HIGHEST,
                preferred_element_type=f32,
            )
        )
    return jnp.concatenate(parts * (LANES // (len(parts) * parts[0].shape[1])), axis=1)


def send_coefs(group_ref, density, basis_ref, coef_ref):
    clusters, rank, _ = basis_ref.shape
    lane = lax.broadcasted_iota(jnp.int32, (1, LANES), 1) // (clusters * rank)
    mine = jnp.where(lane == group_ref[0], coefs_of(density, basis_ref), 0.0)
    coef_ref[...] = jnp.broadcast_to(mine, coef_ref.shape)


def start_kernel(group_ref, recv_ref, basis_ref, rhs_ref, low_ref, coef_ref):
    own, width = rhs_ref.shape
    lines = own * width // LANES
    block = lines * 8 // math.gcd(lines, 8)
    values = recv_ref[...].astype(f32)
    total = sum(values[k : k + block] for k in range(0, values.shape[0], block))
    total = sum(total[k : k + lines] for k in range(0, block, lines))
    rhs = jnp.concatenate(
        [
            jnp.concatenate([total[k : k + 1] for k in range(t, lines, own)], axis=1)
            for t in range(own)
        ],
        axis=0,
    )
    rhs_ref[...] = rhs
    low_ref[...] = rhs.astype(bf16)
    send_coefs(group_ref, rhs, basis_ref, coef_ref)


def near_kernel(pick_ref, blocks_ref, low_ref, other_ref, out_ref):
    clusters, width = out_ref.shape
    other = other_ref[...].astype(f32)
    for t in range(clusters):
        low = low_ref[t : t + 1, :]
        chosen = other[0:1, :]
        for n in range(1, other.shape[0]):
            chosen = jnp.where(pick_ref[t] == n, other[n : n + 1, :], chosen)
        out_ref[t : t + 1, :] = dot_nt(low, blocks_ref[t, 0]) + dot_nt(
            chosen.astype(bf16), blocks_ref[t, 1]
        )


def far_of(index_ref, table_ref, couple_ref, target_ref, t):
    blocks = couple_ref.shape[1]
    total = None
    for b in range(blocks):
        row = table_ref[pl.ds(index_ref[t * blocks + b], 1), :]
        part = couple_ref[t, b] * row
        total = part if total is None else total + part
    mixed = jnp.sum(total, axis=1, keepdims=True)
    return jnp.sum(mixed * target_ref[t], axis=0, keepdims=True)


def step_kernel(
    index_ref, group_ref, table_ref, couple_ref, target_ref, rhs_ref, near_ref, basis_ref, *out_refs
):
    clusters = rhs_ref.shape[0]
    far = jnp.concatenate(
        [far_of(index_ref, table_ref, couple_ref, target_ref, t) for t in range(clusters)], axis=0
    )
    density = rhs_ref[...] - near_ref[...] - far
    if len(out_refs) == 1:
        out_refs[0][...] = density
    else:
        out_refs[0][...] = density.astype(bf16)
        send_coefs(group_ref, density, basis_ref, out_refs[1])


def start(group, received, basis):
    clusters, rank, width = basis.shape
    chips = lax.axis_size(CHIPS)
    return pl.pallas_call(
        start_kernel,
        out_shape=(
            kept((clusters, width), f32),
            kept((clusters, width), bf16),
            kept((chips, LANES), f32),
        ),
        in_specs=[SMEM] + [VMEM] * 2,
        out_specs=(VMEM,) * 3,
        cost_estimate=pl.CostEstimate(flops=500_000, bytes_accessed=400_000, transcendentals=0),
        name="start",
    )(group, *held(received, basis))


def near_part(pick, blocks, low, other):
    return pl.pallas_call(
        near_kernel,
        out_shape=kept(low.shape, f32),
        in_specs=[SMEM, VMEM, VMEM, VMEM],
        out_specs=VMEM,
        cost_estimate=pl.CostEstimate(flops=2_000_000, bytes_accessed=1_200_000, transcendentals=0),
        name="near_part",
    )(pick, *held(blocks, low, other))


def step(index, group, table, couple, target, rhs, near, basis, last):
    clusters, rank, width = basis.shape
    chips = lax.axis_size(CHIPS)
    if last:
        shapes = [jax.ShapeDtypeStruct((clusters, width), f32)]
    else:
        shapes = [kept((clusters, width), bf16), kept((chips, LANES), f32)]
    return pl.pallas_call(
        step_kernel,
        out_shape=tuple(shapes),
        in_specs=[SMEM] * 2 + [VMEM] * 6,
        out_specs=(VMEM,) * len(shapes),
        cost_estimate=pl.CostEstimate(flops=500_000, bytes_accessed=500_000, transcendentals=0),
        name="step",
    )(index, group, *held(table, couple, target, rhs, near, basis))


def local(
    shape_coef,
    force_coef,
    near_cell,
    near_dest,
    near_slot,
    panel_centers,
    near_blocks,
    near_pick,
    src_basis,
    far_couple,
    far_src,
    far_rank,
    tgt_basis,
    cluster_slot,
):
    walls = lax.axis_size(WALL)
    clusters, width = panel_centers.shape
    rank = far_couple.shape[2]
    harmonic = harmonics(ORDER)
    quads = harmonic.shape[0]
    padded = -(-quads // LANES) * LANES
    grid = np.zeros((harmonic.shape[1], padded), np.float32)
    grid[:, :quads] = harmonic.T
    grid = jnp.asarray(grid, f32).astype(bf16)
    harmonic = jnp.asarray(harmonic, f32).astype(bf16)

    centers = gather_wall(panel_centers)
    sources = near_sources(near_cell, shape_coef, force_coef, grid)
    surface = jnp.einsum(
        "qs,asc->aqc", harmonic, shape_coef, preferred_element_type=jnp.float32
    ).astype(bf16)

    basis = jnp.swapaxes(src_basis, 1, 2)

    cores = lax.axis_size(CORE)
    live = -(-quads // 16) * 16
    sums = pair_sums(near_dest, near_slot, sources, centers, live, cores)
    far_src, far_rank, sums = lax.optimization_barrier((far_src, far_rank, sums))
    received = exchange_wall(sums, walls)

    source_rows = jnp.take(cluster_slot, far_src.reshape(-1), axis=0)
    per_row = LANES // rank
    index, offset = table_place(source_rows, clusters, rank)
    levels = jnp.arange(rank, dtype=jnp.int32)
    keep = (levels[None, None, :, None] < far_rank[:, :, None, None]) & (
        levels[None, None, None, :] < far_rank[:, :, None, None]
    )
    masked = jnp.where(keep, far_couple, jnp.zeros_like(far_couple))
    lane_part = jnp.arange(LANES, dtype=jnp.int32) // rank
    here = lane_part[None, None, None, :] == offset.reshape(far_src.shape)[:, :, None, None]
    couple = jnp.where(here, jnp.tile(masked, (1, 1, 1, per_row)), 0.0)
    chips = lax.axis_size(CHIPS)
    groups = LANES // (clusters * rank)
    group = (lax.axis_index(CHIPS) // (chips // groups)).astype(jnp.int32).reshape(1)
    rhs, low, coef = start(group, received, basis)
    for k in range(ITERS):
        other = shifted(low, WALL, 1)
        near = near_part(near_pick, near_blocks, low, other)
        table = gather_all(coef, clusters, rank)
        out = step(index, group, table, couple, tgt_basis, rhs, near, basis, k == ITERS - 1)
        if k < ITERS - 1:
            low, coef = out
        else:
            (density,) = out
    return (surface, density)


def centers_kernel(spots_ref, out_ref):
    own, width = spots_ref.shape
    spots = spots_ref[...] * (FIXED / REACH)
    lines = jnp.concatenate(
        [spots[t : t + 1, k : k + LANES] for k in range(0, width, LANES) for t in range(own)],
        axis=0,
    )
    lines = jnp.clip(jnp.round(lines), -FIXED, FIXED)
    count = lines.shape[0]
    copies = 16 // math.gcd(count, 16)
    block = jnp.concatenate([lines] * copies, axis=0).astype(jnp.int32).astype(jnp.int16)
    for k in range(0, out_ref.shape[0], count * copies):
        out_ref[pl.ds(k, count * copies), :] = block


def gather_wall(panel_centers):
    chips = lax.axis_size(CHIPS)
    clusters, width = panel_centers.shape
    pieces = pl.pallas_call(
        centers_kernel,
        out_shape=jax.ShapeDtypeStruct((chips * clusters * width // LANES, LANES), jnp.int16),
        in_specs=[VMEM],
        out_specs=VMEM,
        cost_estimate=pl.CostEstimate(flops=10_000, bytes_accessed=50_000, transcendentals=0),
        name="centers",
    )(panel_centers)
    pieces = pieces.reshape(-1, clusters, LANES)
    pieces = lax.all_to_all(pieces, CHIPS, split_axis=0, concat_axis=0, tiled=True)
    return lax.all_gather(pieces, CORE).reshape(-1, LANES)


def exchange_wall(sums, walls):
    pieces = sums.reshape(-1, OWN, LANES)
    pieces = lax.all_to_all(pieces, WALL, split_axis=0, concat_axis=0, tiled=True)
    return pieces.reshape(-1, LANES)


def gather_all(coef, clusters, rank):
    chips = lax.axis_size(CHIPS)
    peers = lax.axis_size(PLANE)
    groups = LANES // (clusters * rank)
    pieces = coef.reshape(chips, 1, LANES)
    pieces = lax.all_to_all(pieces, CHIPS, split_axis=0, concat_axis=0, tiled=True)
    own = jnp.sum(pieces.reshape(groups, chips // groups, LANES), axis=0)
    pieces = jnp.broadcast_to(own.reshape(1, 1, -1), (peers, 1, own.size))
    pieces = lax.all_to_all(pieces, PLANE, split_axis=0, concat_axis=0, tiled=True)
    return pieces.reshape(-1, LANES)


def table_place(slots, clusters, rank):
    chips, cores = lax.axis_size(CHIPS), lax.axis_size(CORE)
    groups = LANES // (clusters * rank)
    lines = chips // groups
    device = slots // clusters
    cell, chip, core = device // (chips * cores), device // cores % chips, device % cores
    return (cell * cores + core) * lines + chip % lines, chip // lines * clusters + slots % clusters


def solution(mesh):
    finer = Mesh(mesh.devices.reshape(4, 4, 32, 2), ("cells_0", "cells_1", "wall_0", "wall_1"))
    return jax.shard_map(
        local,
        mesh=finer,
        in_specs=(
            P(None, None, CELLS_WALL),
            P(None, None, CELLS_WALL),
            P(CELLS_WALL),
            P(CELLS_WALL),
            P(CELLS_WALL),
            P(CELLS_WALL, None),
            P(CELLS_WALL, None, None, None),
            P(CELLS_WALL),
            P(CELLS_WALL, None, None),
            P(CELLS_WALL, None, None, None),
            P(CELLS_WALL, None),
            P(CELLS_WALL, None),
            P(CELLS_WALL, None, None),
            P(),
        ),
        out_specs=(P(None, None, CELLS_WALL), P(CELLS_WALL, None)),
        check_vma=False,
    )
```

```python
import functools
import math

import jax
import jax.numpy as jnp
import numpy as np
from jax import lax
from jax.experimental import pallas as pl
from jax.experimental.pallas import tpu as pltpu
from jax.sharding import Mesh
from jax.sharding import PartitionSpec as P

ORDER = 16
ITERS = 2
WALL = ("wall_0", "wall_1")
CHIPS = "wall_0"
CORE = "wall_1"
PLANE = ("cells_0", "cells_1", "wall_1")
CELLS_WALL = ("cells_0", "cells_1", "wall_0", "wall_1")

soft_core = 0.25
stokes_scale = 1.0 / (8.0 * math.pi)
LANES = 128
REACH = 2.0
FIXED = 32767.0
PANELS = 128
OWN = 2
f32 = jnp.float32
bf16 = jnp.bfloat16
VMEM = pl.BlockSpec(memory_space=pltpu.VMEM)
SMEM = pl.BlockSpec(memory_space=pltpu.SMEM)


def shifted(array, axis, by):
    devices = lax.axis_size(axis)
    return lax.ppermute(array, axis, [(i, (i + by) % devices) for i in range(devices)])


def harmonics(order):
    lat_count = order + 1
    polar_angle = np.pi * (np.arange(lat_count) + 0.5) / lat_count
    azimuth = np.pi * np.arange(2 * lat_count) / lat_count
    cos_polar = np.repeat(np.cos(polar_angle), 2 * lat_count)
    sin_polar = np.repeat(np.sin(polar_angle), 2 * lat_count)
    az_grid = np.tile(azimuth, lat_count)
    legendre = {}
    legendre[0, 0] = cos_polar * 0.0 + 0.5 / np.sqrt(np.pi)
    for m in range(1, order + 1):
        legendre[m, m] = -np.sqrt((2.0 * m + 1.0) / (2.0 * m)) * sin_polar * legendre[m - 1, m - 1]
    for m in range(order):
        legendre[m + 1, m] = np.sqrt(2.0 * m + 3.0) * cos_polar * legendre[m, m]
    for m in range(order + 1):
        for l in range(m + 2, order + 1):
            factor = np.sqrt((4.0 * l * l - 1.0) / (l * l - m * m))
            backward = np.sqrt(((l - 1.0) ** 2 - m * m) / (4.0 * (l - 1.0) ** 2 - 1.0))
            legendre[l, m] = factor * (
                cos_polar * legendre[l - 1, m] - backward * legendre[l - 2, m]
            )
    columns = []
    for l in range(order + 1):
        for m in range(-l, l + 1):
            if m > 0:
                columns.append(np.sqrt(2.0) * legendre[l, m] * np.cos(m * az_grid))
            elif m < 0:
                columns.append(np.sqrt(2.0) * legendre[l, -m] * np.sin(-m * az_grid))
            else:
                columns.append(legendre[l, 0])
    return np.stack(columns, axis=1)


def kept(shape, dtype):
    return pltpu.VMEM(shape, dtype)


def held(*arrays):
    return [pltpu.with_memory_space_constraint(array, pltpu.VMEM) for array in arrays]


def dot_nn(a, b):
    return lax.dot_general(a, b, (((1,), (0,)), ((), ())), preferred_element_type=f32)


def dot_nt(a, b):
    return lax.dot_general(a, b, (((1,), (1,)), ((), ())), preferred_element_type=f32)


def dot_tn(a, b):
    return lax.dot_general(a, b, (((0,), (0,)), ((), ())), preferred_element_type=f32)


def split3(value):
    high = value.astype(bf16).astype(f32)
    rest = value - high
    middle = rest.astype(bf16).astype(f32)
    return high, middle, rest - middle


def sources_kernel(cell_ref, shape_ref, force_ref, grid_ref, out_ref):
    rows = out_ref.shape[1]
    cells = shape_ref.shape[2]
    pick = (lax.broadcasted_iota(jnp.int32, (cells, rows), 0) == cell_ref[...]).astype(f32)
    pick = jnp.transpose(pick).astype(bf16)
    for base, ref in ((0, shape_ref), (3, force_ref)):
        for a in range(3):
            coefs = dot_nt(pick, ref[a]).astype(bf16)
            out_ref[base + a] = dot_nn(coefs, grid_ref[...]).astype(bf16)


def near_sources(near_cell, shape_coef, force_coef, grid):
    rows = near_cell.shape[0]
    return pl.pallas_call(
        sources_kernel,
        out_shape=kept((6, rows, grid.shape[1]), bf16),
        in_specs=[VMEM] * 4,
        out_specs=VMEM,
        cost_estimate=pl.CostEstimate(flops=200_000_000, bytes_accessed=2_500_000, transcendentals=0),
        name="near_sources",
    )(near_cell.reshape(1, rows), shape_coef, force_coef, grid)


def put(ref, k, value):
    rows = value.shape[0]
    for j in range(ref.shape[0]):
        ref[j, pl.ds(k * rows, rows), :] = value[:, j * LANES : (j + 1) * LANES]


def get(ref, r, rows):
    return jnp.concatenate(
        [ref[j, pl.ds(r, 16, stride=rows), :] for j in range(ref.shape[0])], axis=1
    )


def pairs_kernel(
    cores, dest_ref, slot_ref, src_ref, ctr_ref, out_ref, ysc, gsc, bsc, mom, xsc, csc, *bufs
):
    rows, quads = src_ref.shape[1], src_ref.shape[2]
    lines = OWN * 3
    walls = out_ref.shape[0] // lines
    half = len(bufs) // 2
    rho_bufs, pow_bufs = bufs[:half], bufs[half:]
    pan = PANELS
    own = OWN
    clusters = walls * own
    dest, slot = dest_ref[...], slot_ref[...]
    chips = walls // cores
    place = slot * walls + lax.rem(dest, cores) * chips + lax.div(dest, cores)
    target = slot * walls + dest
    y = [src_ref[a].astype(f32) for a in range(3)]
    f = [src_ref[3 + a].astype(f32) for a in range(3)]
    y2 = y[0] * y[0] + y[1] * y[1] + y[2] * y[2]
    yf = y[0] * f[0] + y[1] * f[1] + y[2] * f[2]
    for k in range(9):
        put(ysc, k, -2.0 * y[k % 3])
    for k, piece in enumerate(split3(y2)):
        put(ysc, 9 + k, piece)
    for k in range(12, 15):
        put(ysc, k, jnp.ones((rows, quads), f32))
    put(ysc, 15, jnp.zeros((rows, quads), f32))
    for b in range(3):
        put(gsc, b, f[b])
    put(gsc, 3, yf)
    for a in range(3):
        for b in range(3):
            put(gsc, 4 + 3 * a + b, y[a] * f[b])
        put(gsc, 13 + a, y[a] * yf)
    csc[...] = ctr_ref[...].astype(jnp.int32).astype(f32) * (REACH / FIXED)
    pick = (lax.broadcasted_iota(jnp.int32, (clusters, rows), 0) == place).astype(f32)
    pick = jnp.transpose(pick).astype(bf16)
    x = []
    for a in range(3):
        total = None
        spots = jnp.concatenate(
            [csc[pl.ds(own * a + t, walls, stride=lines), :] for t in range(own)], axis=0
        )
        for i, piece in enumerate(split3(spots)):
            part = dot_nn(pick, piece.astype(bf16))
            bsc[pl.ds((3 * i + a) * rows, rows), :] = part
            total = part if total is None else total + part
        x.append(total)
        xsc[pl.ds(a * rows, rows), :] = total
    x2 = x[0] * x[0] + x[1] * x[1] + x[2] * x[2] + soft_core
    for k in range(9, 12):
        bsc[pl.ds(k * rows, rows), :] = jnp.ones((rows, pan), f32)
    for k, piece in enumerate(split3(x2)):
        bsc[pl.ds((12 + k) * rows, rows), :] = piece
    bsc[pl.ds(15 * rows, rows), :] = jnp.zeros((rows, pan), f32)

    lanes = len(rho_bufs) // 2

    def turn(i, old, new):
        held_pow, next_pow = pow_bufs[old::2], pow_bufs[new::2]
        held_rho, next_rho = rho_bufs[old::2], rho_bufs[new::2]
        for n in range(lanes):
            r = jnp.clip(lanes * (i - 2) + n, n, rows - lanes + n)
            g = get(gsc, r, rows)
            g_hi = g.astype(bf16)
            g_lo = (g - g_hi.astype(f32)).astype(bf16)
            both = jnp.concatenate([g_hi, g_lo], axis=0)
            sums = jnp.transpose(dot_nt(held_pow[n][...], both))
            mom[pl.ds(r, 16, stride=rows), :] = sums[:16, :pan] + sums[16:, :pan]
            mom[pl.ds(16 * rows + r, 8, stride=rows), :] = sums[:8, pan:]
        for n in range(lanes):
            inverse = lax.rsqrt(held_rho[n][...])
            next_pow[n][pl.ds(0, pan), :] = (inverse * inverse * inverse).astype(bf16)
            next_pow[n][pl.ds(pan, pan), :] = inverse.astype(bf16)
        for n in range(lanes):
            r = jnp.minimum(lanes * i + n, rows - lanes + n)
            yr = get(ysc, r, rows).astype(bf16)
            br = bsc[pl.ds(r, 16, stride=rows), :].astype(bf16)
            next_rho[n][...] = dot_tn(br, yr)

    def turns(i, carry):
        turn(2 * i, 0, 1)
        turn(2 * i + 1, 1, 0)
        return carry

    lax.fori_loop(0, (rows // lanes + 2 + 1) // 2, turns, 0, unroll=TURN_UNROLL)
    x = [xsc[pl.ds(a * rows, rows), :] for a in range(3)]
    moment = [mom[pl.ds(c * rows, rows), :] for c in range(19)]
    common = x[0] * moment[0] + x[1] * moment[1] + x[2] * moment[2] - moment[3]
    drop = (lax.broadcasted_iota(jnp.int32, (clusters, rows), 0) == target).astype(bf16)
    for a in range(3):
        local_part = x[0] * moment[4 + 3 * a] + x[1] * moment[5 + 3 * a] + x[2] * moment[6 + 3 * a]
        velocity = moment[16 + a] + x[a] * common - (local_part - moment[13 + a])
        velocity = velocity * (-stokes_scale)
        total = None
        for piece in split3(velocity):
            part = dot_nn(drop, piece.astype(bf16))
            total = part if total is None else total + part
        for t in range(own):
            part = total[t * walls : (t + 1) * walls, :]
            csc[pl.ds(own * a + t, walls, stride=lines), :] = part
    out_ref[...] = csc[...].astype(out_ref.dtype)


PAIR_LANES = 2
TURN_UNROLL = 4


def pair_sums(dest, slot, sources, centers, cores):
    rows, quads = sources.shape[1:]
    pan = PANELS
    return pl.pallas_call(
        functools.partial(pairs_kernel, cores),
        out_shape=jax.ShapeDtypeStruct(centers.shape, bf16),
        in_specs=[VMEM] * 4,
        out_specs=VMEM,
        scratch_shapes=[
            pltpu.VMEM((quads // LANES, 16 * rows, LANES), f32),
            pltpu.VMEM((quads // LANES, 16 * rows, LANES), f32),
            pltpu.VMEM((16 * rows, pan), f32),
            pltpu.VMEM((24 * rows, pan), f32),
            pltpu.VMEM((3 * rows, pan), f32),
            pltpu.VMEM(centers.shape, f32),
        ]
        + [pltpu.VMEM((pan, quads), f32)] * (2 * PAIR_LANES)
        + [pltpu.VMEM((2 * pan, quads), bf16)] * (2 * PAIR_LANES),
        cost_estimate=pl.CostEstimate(
            flops=1_000_000_000, bytes_accessed=1_000_000, transcendentals=5_000_000
        ),
        name="pair_sums",
    )(*held(dest.reshape(1, rows), slot.reshape(1, rows), sources, centers))


def coefs_of(density, basis_ref):
    parts = []
    for t in range(density.shape[0]):
        parts.append(
            lax.dot_general(
                density[t : t + 1, :],
                basis_ref[t],
                (((1,), (1,)), ((), ())),
                precision=lax.Precision.HIGHEST,
                preferred_element_type=f32,
            )
        )
    return jnp.concatenate(parts * (LANES // (len(parts) * parts[0].shape[1])), axis=1)


def send_coefs(group_ref, density, basis_ref, coef_ref):
    clusters, rank, _ = basis_ref.shape
    lane = lax.broadcasted_iota(jnp.int32, (1, LANES), 1) // (clusters * rank)
    mine = jnp.where(lane == group_ref[0], coefs_of(density, basis_ref), 0.0)
    coef_ref[...] = jnp.broadcast_to(mine, coef_ref.shape)


def start_kernel(group_ref, recv_ref, basis_ref, rhs_ref, low_ref, coef_ref):
    own, width = rhs_ref.shape
    lines = own * width // LANES
    block = lines * 8 // math.gcd(lines, 8)
    values = recv_ref[...].astype(f32)
    total = sum(values[k : k + block] for k in range(0, values.shape[0], block))
    total = sum(total[k : k + lines] for k in range(0, block, lines))
    rhs = jnp.concatenate(
        [
            jnp.concatenate([total[k : k + 1] for k in range(t, lines, own)], axis=1)
            for t in range(own)
        ],
        axis=0,
    )
    rhs_ref[...] = rhs
    low_ref[...] = rhs.astype(bf16)
    send_coefs(group_ref, rhs, basis_ref, coef_ref)


def near_kernel(pick_ref, blocks_ref, low_ref, other_ref, out_ref):
    clusters, width = out_ref.shape
    other = other_ref[...].astype(f32)
    for t in range(clusters):
        low = low_ref[t : t + 1, :]
        chosen = other[0:1, :]
        for n in range(1, other.shape[0]):
            chosen = jnp.where(pick_ref[t] == n, other[n : n + 1, :], chosen)
        out_ref[t : t + 1, :] = dot_nt(low, blocks_ref[t, 0]) + dot_nt(
            chosen.astype(bf16), blocks_ref[t, 1]
        )


def far_of(index_ref, table_ref, couple_ref, target_ref, t):
    blocks = couple_ref.shape[1]
    total = None
    for b in range(blocks):
        row = table_ref[pl.ds(index_ref[t * blocks + b], 1), :]
        part = couple_ref[t, b] * row
        total = part if total is None else total + part
    mixed = jnp.sum(total, axis=1, keepdims=True)
    return jnp.sum(mixed * target_ref[t], axis=0, keepdims=True)


def step_kernel(
    index_ref, group_ref, table_ref, couple_ref, target_ref, rhs_ref, near_ref, basis_ref, *out_refs
):
    clusters = rhs_ref.shape[0]
    far = jnp.concatenate(
        [far_of(index_ref, table_ref, couple_ref, target_ref, t) for t in range(clusters)], axis=0
    )
    density = rhs_ref[...] - near_ref[...] - far
    if len(out_refs) == 1:
        out_refs[0][...] = density
    else:
        out_refs[0][...] = density.astype(bf16)
        send_coefs(group_ref, density, basis_ref, out_refs[1])


def start(group, received, basis):
    clusters, rank, width = basis.shape
    chips = lax.axis_size(CHIPS)
    return pl.pallas_call(
        start_kernel,
        out_shape=(
            kept((clusters, width), f32),
            kept((clusters, width), bf16),
            kept((chips, LANES), f32),
        ),
        in_specs=[SMEM] + [VMEM] * 2,
        out_specs=(VMEM,) * 3,
        cost_estimate=pl.CostEstimate(flops=500_000, bytes_accessed=400_000, transcendentals=0),
        name="start",
    )(group, *held(received, basis))


def near_part(pick, blocks, low, other):
    return pl.pallas_call(
        near_kernel,
        out_shape=kept(low.shape, f32),
        in_specs=[SMEM, VMEM, VMEM, VMEM],
        out_specs=VMEM,
        cost_estimate=pl.CostEstimate(flops=2_000_000, bytes_accessed=1_200_000, transcendentals=0),
        name="near_part",
    )(pick, *held(blocks, low, other))


def step(index, group, table, couple, target, rhs, near, basis, last):
    clusters, rank, width = basis.shape
    chips = lax.axis_size(CHIPS)
    if last:
        shapes = [jax.ShapeDtypeStruct((clusters, width), f32)]
    else:
        shapes = [kept((clusters, width), bf16), kept((chips, LANES), f32)]
    return pl.pallas_call(
        step_kernel,
        out_shape=tuple(shapes),
        in_specs=[SMEM] * 2 + [VMEM] * 6,
        out_specs=(VMEM,) * len(shapes),
        cost_estimate=pl.CostEstimate(flops=500_000, bytes_accessed=500_000, transcendentals=0),
        name="step",
    )(index, group, *held(table, couple, target, rhs, near, basis))


def local(
    shape_coef,
    force_coef,
    near_cell,
    near_dest,
    near_slot,
    panel_centers,
    near_blocks,
    near_pick,
    src_basis,
    far_couple,
    far_src,
    far_rank,
    tgt_basis,
    cluster_slot,
):
    walls = lax.axis_size(WALL)
    clusters, width = panel_centers.shape
    rank = far_couple.shape[2]
    harmonic = harmonics(ORDER)
    quads = harmonic.shape[0]
    padded = -(-quads // LANES) * LANES
    grid = np.zeros((harmonic.shape[1], padded), np.float32)
    grid[:, :quads] = harmonic.T
    grid = jnp.asarray(grid, f32).astype(bf16)
    harmonic = jnp.asarray(harmonic, f32).astype(bf16)

    centers = gather_wall(panel_centers)
    sources = near_sources(near_cell, shape_coef, force_coef, grid)
    surface = jnp.einsum(
        "qs,asc->aqc", harmonic, shape_coef, preferred_element_type=jnp.float32
    ).astype(bf16)

    basis = jnp.swapaxes(src_basis, 1, 2)

    cores = lax.axis_size(CORE)
    sums = pair_sums(near_dest, near_slot, sources, centers, cores)
    far_src, far_rank, sums = lax.optimization_barrier((far_src, far_rank, sums))
    received = exchange_wall(sums, walls)

    source_rows = jnp.take(cluster_slot, far_src.reshape(-1), axis=0)
    per_row = LANES // rank
    index, offset = table_place(source_rows, clusters, rank)
    levels = jnp.arange(rank, dtype=jnp.int32)
    keep = (levels[None, None, :, None] < far_rank[:, :, None, None]) & (
        levels[None, None, None, :] < far_rank[:, :, None, None]
    )
    masked = jnp.where(keep, far_couple, jnp.zeros_like(far_couple))
    lane_part = jnp.arange(LANES, dtype=jnp.int32) // rank
    here = lane_part[None, None, None, :] == offset.reshape(far_src.shape)[:, :, None, None]
    couple = jnp.where(here, jnp.tile(masked, (1, 1, 1, per_row)), 0.0)
    chips = lax.axis_size(CHIPS)
    groups = LANES // (clusters * rank)
    group = (lax.axis_index(CHIPS) // (chips // groups)).astype(jnp.int32).reshape(1)
    rhs, low, coef = start(group, received, basis)
    for k in range(ITERS):
        other = shifted(low, WALL, 1)
        near = near_part(near_pick, near_blocks, low, other)
        table = gather_all(coef, clusters, rank)
        out = step(index, group, table, couple, tgt_basis, rhs, near, basis, k == ITERS - 1)
        if k < ITERS - 1:
            low, coef = out
        else:
            (density,) = out
    return (surface, density)


def centers_kernel(spots_ref, out_ref):
    own, width = spots_ref.shape
    spots = spots_ref[...] * (FIXED / REACH)
    lines = jnp.concatenate(
        [spots[t : t + 1, k : k + LANES] for k in range(0, width, LANES) for t in range(own)],
        axis=0,
    )
    lines = jnp.clip(jnp.round(lines), -FIXED, FIXED)
    count = lines.shape[0]
    copies = 16 // math.gcd(count, 16)
    block = jnp.concatenate([lines] * copies, axis=0).astype(jnp.int32).astype(jnp.int16)
    for k in range(0, out_ref.shape[0], count * copies):
        out_ref[pl.ds(k, count * copies), :] = block


def gather_wall(panel_centers):
    chips = lax.axis_size(CHIPS)
    clusters, width = panel_centers.shape
    pieces = pl.pallas_call(
        centers_kernel,
        out_shape=jax.ShapeDtypeStruct((chips * clusters * width // LANES, LANES), jnp.int16),
        in_specs=[VMEM],
        out_specs=VMEM,
        cost_estimate=pl.CostEstimate(flops=10_000, bytes_accessed=50_000, transcendentals=0),
        name="centers",
    )(panel_centers)
    pieces = pieces.reshape(-1, clusters, LANES)
    pieces = lax.all_to_all(pieces, CHIPS, split_axis=0, concat_axis=0, tiled=True)
    return lax.all_gather(pieces, CORE).reshape(-1, LANES)


def exchange_wall(sums, walls):
    pieces = sums.reshape(-1, OWN, LANES)
    pieces = lax.all_to_all(pieces, WALL, split_axis=0, concat_axis=0, tiled=True)
    return pieces.reshape(-1, LANES)


def gather_all(coef, clusters, rank):
    chips = lax.axis_size(CHIPS)
    peers = lax.axis_size(PLANE)
    groups = LANES // (clusters * rank)
    pieces = coef.reshape(chips, 1, LANES)
    pieces = lax.all_to_all(pieces, CHIPS, split_axis=0, concat_axis=0, tiled=True)
    own = jnp.sum(pieces.reshape(groups, chips // groups, LANES), axis=0)
    pieces = jnp.broadcast_to(own.reshape(1, 1, -1), (peers, 1, own.size))
    pieces = lax.all_to_all(pieces, PLANE, split_axis=0, concat_axis=0, tiled=True)
    return pieces.reshape(-1, LANES)


def table_place(slots, clusters, rank):
    chips, cores = lax.axis_size(CHIPS), lax.axis_size(CORE)
    groups = LANES // (clusters * rank)
    lines = chips // groups
    device = slots // clusters
    cell, chip, core = device // (chips * cores), device // cores % chips, device % cores
    return (cell * cores + core) * lines + chip % lines, chip // lines * clusters + slots % clusters


def solution(mesh):
    finer = Mesh(mesh.devices.reshape(4, 4, 32, 2), ("cells_0", "cells_1", "wall_0", "wall_1"))
    return jax.shard_map(
        local,
        mesh=finer,
        in_specs=(
            P(None, None, CELLS_WALL),
            P(None, None, CELLS_WALL),
            P(CELLS_WALL),
            P(CELLS_WALL),
            P(CELLS_WALL),
            P(CELLS_WALL, None),
            P(CELLS_WALL, None, None, None),
            P(CELLS_WALL),
            P(CELLS_WALL, None, None),
            P(CELLS_WALL, None, None, None),
            P(CELLS_WALL, None),
            P(CELLS_WALL, None),
            P(CELLS_WALL, None, None),
            P(),
        ),
        out_specs=(P(None, None, CELLS_WALL), P(CELLS_WALL, None)),
        check_vma=False,
    )
```
